256 devices in a mesh: head: 8 (over y, core), ctx: 32 (over x, z).
Axes of the slice: x: 4, y: 4, z: 8, core: 2. Of those that a mesh axis runs over, the one named last changes fastest.
Arguments:
- main_queries: bfloat16 [512, 128, 192], P(None, 'head'), may hold values from -6 to 6
- main_keys: bfloat16 [32768, 128, 192], P('ctx', 'head'), may hold values from -7 to 7
- log_sums: float32 [512, 128], P(None, 'head'), may hold values from 10 to 13
- index_queries: bfloat16 [512, 64, 128], P('head'), may hold values from -2 to 2
- index_weights: bfloat16 [512, 64], P('head'), may hold values from -3 to 3
- index_keys: bfloat16 [32768, 128], P('ctx'), may hold values from -7 to 7
- loss_weights: float32 [512], P('head'), may hold values from 4 to 64
Outputs:
- query_grad: bfloat16 [512, 64, 128], P('head', 'ctx')
- weight_grad: float32 [512, 64], P('head', 'ctx')
- key_grad: bfloat16 [32768, 128], P('ctx', 'head')
The draws below stay inside these ranges and needn't reach their ends.
All inputs are finite; a program needn't handle non-finite values.
Results may differ from the reference program's by a relative error of at most 0.023.
Values may be sent and summed in bfloat16 or wider, within the bound.
No kernel may reach another device: no remote copies, remote signals or barrier semaphores. Data moves between devices by JAX's collectives and lax.ppermute only.
A program may use at most 128 MiB of HBM per device.

```python
import math
import jax
import jax.numpy as jnp
from jax import lax

H = 128
DS = 192
IH = 64
ID = 128
QUERIES = 512
KEYS = 32768
N_HEAD = 8


def indexer_fields(key):
    base = jax.random.fold_in(key, 71)
    key_one, key_two, key_three = jax.random.split(base, 3)
    position = jnp.arange(KEYS, dtype=jnp.float32) / KEYS
    rising = 0.5 + 1.5 * position
    keys = jnp.clip(jax.random.normal(key_one, (KEYS, ID), jnp.float32), -3.5, 3.5) * rising[:, None]
    queries = jnp.clip(jax.random.normal(key_two, (QUERIES, IH, ID), jnp.float32), -4.0, 4.0) * ID ** (-0.5)
    weights = jnp.clip(jax.random.normal(key_three, (QUERIES, IH), jnp.float32), -4.0, 4.0) * 0.14
    return (queries, keys, weights)


def draw_index_queries(key, part):
    return indexer_fields(key)[0].astype(jnp.bfloat16)


def draw_index_keys(key, part):
    return indexer_fields(key)[1].astype(jnp.bfloat16)


def draw_index_weights(key, part):
    return indexer_fields(key)[2].astype(jnp.bfloat16)


def draw_main_queries(key, part):
    noise_key = jax.random.fold_in(key, 41)
    values = jnp.clip(jax.random.normal(noise_key, (QUERIES, H, DS), jnp.float32), -6.0, 6.0)
    return values.astype(jnp.bfloat16)


def draw_main_keys(key, part):
    key_one = jax.random.fold_in(jax.random.fold_in(key, 29), 0)
    rising = 0.6 + jnp.arange(KEYS, dtype=jnp.float32) / KEYS
    values = jnp.clip(jax.random.normal(key_one, (KEYS, H, DS), jnp.float32), -4.0, 4.0) * rising[:, None, None]
    return values.astype(jnp.bfloat16)


def levels(stream_key, dims, cuts, least, high):
    loudness, own = 1.0, jax.random.fold_in(stream_key, 6)
    for axis_at, blocks in cuts:
        draws = jnp.exp(jax.random.uniform(jax.random.fold_in(own, axis_at), (blocks,), jnp.float32, least / len(cuts), high / len(cuts)))
        loudness = loudness * jnp.repeat(draws, dims[axis_at] // blocks).reshape([-1 if axis == axis_at else 1 for axis in range(len(dims))])
    return loudness


def setup_inputs(seed: int = 0) -> dict:
    seeds = jax.random.split(jax.random.key(seed), 8)
    return {
        "main_queries": draw_main_queries(jax.random.fold_in(seeds[7], 71), 0),
        "main_keys": draw_main_keys(jax.random.fold_in(seeds[7], 71), 0),
        "log_sums": jnp.clip(10.0 + 3.0 * jax.random.uniform(seeds[2], (QUERIES, H), jnp.float32) ** levels(seeds[2], (QUERIES, H), ((1, 8),), -0.2, 0.2), 10.0, 13.0),
        "index_queries": draw_index_queries(jax.random.fold_in(seeds[7], 71), 0),
        "index_weights": draw_index_weights(jax.random.fold_in(seeds[7], 71), 0),
        "index_keys": draw_index_keys(jax.random.fold_in(seeds[7], 71), 0),
        "loss_weights": jnp.clip(jnp.exp(math.log(64.0) - 2.7725887 * jax.random.uniform(seeds[6], (QUERIES,), jnp.float32) ** levels(seeds[6], (QUERIES,), ((0, 8),), -0.2, 0.2)), 4.0, 64.0),
    }


def reference(main_queries, main_keys, log_sums, index_queries, index_weights, index_keys, loss_weights):
    score_scale = DS ** -0.5
    group_heads = H // N_HEAD
    block_rows = 8

    def head_prob(running, head_index):
        queries_one = lax.dynamic_index_in_dim(main_queries, head_index, 1, keepdims=False).astype(jnp.float32)
        keys_one = lax.dynamic_index_in_dim(main_keys, head_index, 1, keepdims=False).astype(jnp.float32)
        logs_one = lax.dynamic_index_in_dim(log_sums, head_index, 1, keepdims=False)
        scores = jnp.dot(queries_one, keys_one.T, preferred_element_type=jnp.float32) * score_scale
        return running + jnp.exp(scores - logs_one[:, None]), None

    def group_prob(running, group_index):
        head_list = group_index * group_heads + jnp.arange(group_heads, dtype=jnp.int32)
        partial_sum, ignored = lax.scan(head_prob, jnp.zeros((QUERIES, KEYS), jnp.float32), head_list)
        rounded = lax.optimization_barrier(partial_sum.astype(jnp.bfloat16))
        return running + rounded.astype(jnp.float32), None

    probs, ignored = lax.scan(group_prob, jnp.zeros((QUERIES, KEYS), jnp.float32), jnp.arange(N_HEAD, dtype=jnp.int32))
    keys_wide = index_keys.astype(jnp.float32)

    def query_block(key_total, block_index):
        first_row = (block_index * block_rows).astype(jnp.int32)
        queries_block = lax.dynamic_slice_in_dim(index_queries, first_row, block_rows, 0).astype(jnp.float32).reshape(block_rows * IH, ID)
        weights_block = lax.dynamic_slice_in_dim(index_weights, first_row, block_rows, 0).astype(jnp.float32)
        probs_block = lax.dynamic_slice_in_dim(probs, first_row, block_rows, 0)
        scale_block = lax.dynamic_slice_in_dim(loss_weights, first_row, block_rows, 0)
        raw_scores = jnp.dot(queries_block, keys_wide.T, preferred_element_type=jnp.float32).reshape(block_rows, IH, KEYS)
        positive = jnp.maximum(raw_scores, 0.0)
        logits = jnp.sum(weights_block[:, :, None] * positive, axis=1)
        row_top = jnp.max(logits, axis=1, keepdims=True)
        expo = jnp.exp(logits - row_top)
        soft_share = expo / jnp.sum(expo, axis=1, keepdims=True)
        target = probs_block / jnp.sum(probs_block, axis=1, keepdims=True)
        grad_rounded = lax.optimization_barrier((scale_block[:, None] * (soft_share - target)).astype(jnp.bfloat16))
        grad_logits = grad_rounded.astype(jnp.float32)
        weight_part = jnp.sum(grad_logits[:, None, :] * positive, axis=2)
        gated_rounded = lax.optimization_barrier(jnp.where(raw_scores > 0, grad_logits[:, None, :] * weights_block[:, :, None], 0.0).astype(jnp.bfloat16))
        gated_flat = gated_rounded.astype(jnp.float32).reshape(block_rows * IH, KEYS)
        query_part = jnp.dot(gated_flat, keys_wide, preferred_element_type=jnp.float32).reshape(block_rows, IH, ID)
        key_total = key_total + jnp.dot(gated_flat.T, queries_block, preferred_element_type=jnp.float32)
        return key_total, (query_part.astype(jnp.bfloat16), weight_part)

    key_total, (query_parts, weight_parts) = lax.scan(query_block, jnp.zeros((KEYS, ID), jnp.float32), jnp.arange(QUERIES // block_rows, dtype=jnp.int32))
    query_grad = query_parts.reshape(QUERIES, IH, ID)
    weight_grad = weight_parts.reshape(QUERIES, IH)
    return query_grad, weight_grad, key_total.astype(jnp.bfloat16)
```

```python
import functools
import math

import jax
import jax.numpy as jnp
from jax import lax
from jax.experimental import pallas as pl
from jax.experimental.pallas import tpu as pltpu
from jax.sharding import Mesh, PartitionSpec as P

F32 = jnp.float32
BF16 = jnp.bfloat16
NY, NC, NX, NZ = 4, 2, 4, 8
MIB = 1 << 20


def rotate(array, axis, shift):
    n = lax.axis_size(axis)
    return lax.ppermute(array, axis, [(i, (i + shift) % n) for i in range(n)])


def score_kernel(place, queries, keys, logs, keep, send, total, *, heads, rows, scale):
    head = pl.program_id(0)

    @pl.when(head == 0)
    def _():
        total[...] = jnp.zeros_like(total)

    depth = queries.shape[1]
    cols = queries.shape[2]
    log_row = logs[0] * (-1.0 / scale)
    high = log_row.astype(BF16).astype(F32)
    rest = log_row - high
    middle = rest.astype(BF16).astype(F32)
    low = rest - middle
    line = lax.broadcasted_iota(jnp.int32, (16, cols), 0)
    extra = jnp.where(
        line == 0, high, jnp.where(line == 1, middle, jnp.where(line == 2, low, 0.0))
    ).astype(BF16)
    left = jnp.concatenate([queries[0], extra], axis=0).T
    right = jnp.concatenate([keys[0], jnp.ones((16, keys.shape[2]), BF16)], axis=0)
    factor = scale * math.log2(math.e)
    tile = 128
    for at in range(0, cols, tile):
        scores = jnp.dot(left[at : at + tile], right, preferred_element_type=F32)
        total[at : at + tile, :] += jnp.exp2(scores * factor)

    @pl.when(head == heads - 1)
    def _():
        y, core = place[0], place[1]
        for r in range(NY):
            base = lax.rem(y + r, NY) * (NC * rows)
            mine = pl.multiple_of(base + core * rows, rows)
            other = pl.multiple_of(base + (1 - core) * rows, rows)
            keep[r] = total[pl.ds(mine, rows), :].astype(BF16)
            send[r] = total[pl.ds(other, rows), :].astype(BF16)


def head_scores(place, queries, keys, logs, rows, scale):
    heads, depth, count = queries.shape
    width = keys.shape[2]
    out = jax.ShapeDtypeStruct((NY, rows, width), BF16)
    whole = pl.BlockSpec((NY, rows, width), lambda h, p: (0, 0, 0))
    return pl.pallas_call(
        functools.partial(score_kernel, heads=heads, rows=rows, scale=scale),
        grid_spec=pltpu.PrefetchScalarGridSpec(
            num_scalar_prefetch=1,
            grid=(heads,),
            in_specs=[
                pl.BlockSpec((1, depth, count), lambda h, p: (h, 0, 0)),
                pl.BlockSpec((1, depth, width), lambda h, p: (h, 0, 0)),
                pl.BlockSpec((1, 1, count), lambda h, p: (h, 0, 0)),
            ],
            out_specs=[whole, whole],
            scratch_shapes=[pltpu.VMEM((count, width), F32)],
        ),
        out_shape=[out, out],
        compiler_params=pltpu.CompilerParams(vmem_limit_bytes=32 * MIB),
        cost_estimate=pl.CostEstimate(
            flops=2 * heads * depth * count * width,
            bytes_accessed=12 * MIB,
            transcendentals=heads * count * width,
        ),
        name="head_scores",
    )(place, queries, keys, logs[:, None, :])


def logit_kernel(queries, keys, weights, logits, mask, *, group):
    step = pl.program_id(0)
    rows = queries.shape[1]

    @pl.when(step == 0)
    def _():
        logits[...] = jnp.zeros_like(logits)

    for k in range(group):
        raw = lax.dot_general(
            queries[k], keys[...], (((1,), (1,)), ((), ())), preferred_element_type=F32
        )
        mask[k] = jnp.where(raw > 0, 1.0, 0.0).astype(BF16)
        logits[...] += weights[k] * jnp.maximum(raw, 0.0)


def index_logits(queries, keys, weights):
    heads, rows, depth = queries.shape
    width = keys.shape[0]
    group = 8
    return pl.pallas_call(
        functools.partial(logit_kernel, group=group),
        grid=(heads // group,),
        in_specs=[
            pl.BlockSpec((group, rows, depth), lambda i: (i, 0, 0)),
            pl.BlockSpec((width, depth), lambda i: (0, 0)),
            pl.BlockSpec((group, rows, 1), lambda i: (i, 0, 0)),
        ],
        out_specs=[
            pl.BlockSpec((rows, width), lambda i: (0, 0)),
            pl.BlockSpec((group, rows, width), lambda i: (i, 0, 0)),
        ],
        out_shape=[
            jax.ShapeDtypeStruct((rows, width), F32),
            jax.ShapeDtypeStruct((heads, rows, width), BF16),
        ],
        compiler_params=pltpu.CompilerParams(vmem_limit_bytes=32 * MIB),
        cost_estimate=pl.CostEstimate(
            flops=2 * heads * rows * depth * width,
            bytes_accessed=10 * MIB,
            transcendentals=0,
        ),
        name="index_logits",
    )(queries, keys, weights)


def stats_kernel(logits, one, two, three, four, probs, stats):
    summed = (
        one[...].astype(F32) + two[...].astype(F32) + three[...].astype(F32) + four[...].astype(F32)
    )
    probs[...] = summed
    values = logits[...]
    top = jnp.max(values, axis=1, keepdims=True)
    total = jnp.sum(jnp.exp(values - top), axis=1, keepdims=True)
    mass = jnp.sum(summed, axis=1, keepdims=True)
    lane = lax.broadcasted_iota(jnp.int32, (values.shape[0], 128), 1)
    packed = jnp.where(lane == 0, top, jnp.where(lane == 1, total, jnp.where(lane == 2, mass, 0.0)))
    stats[...] = packed.T[:8]


def local_stats(logits, parts):
    rows, width = logits.shape
    return pl.pallas_call(
        stats_kernel,
        out_shape=[
            jax.ShapeDtypeStruct((rows, width), F32),
            jax.ShapeDtypeStruct((8, rows), F32),
        ],
        compiler_params=pltpu.CompilerParams(vmem_limit_bytes=16 * MIB),
        name="local_stats",
    )(logits, *parts)


def grad_kernel(place, logits, probs, stats, loss, mask, keys, scaled, query_part, key_part, grads, total, *, steps):
    step = pl.program_id(0)
    rows = logits.shape[0]

    @pl.when(step == 0)
    def _():
        each = stats[...]
        tops = each[:, 0, :]
        top = jnp.max(tops, axis=0, keepdims=True)
        denominator = jnp.sum(each[:, 1, :] * jnp.exp(tops - top), axis=0, keepdims=True)
        mass = jnp.sum(each[:, 2, :], axis=0, keepdims=True)
        line = lax.broadcasted_iota(jnp.int32, (128, rows), 0)
        packed = jnp.where(
            line == 0,
            top,
            jnp.where(line == 1, denominator, jnp.where(line == 2, mass, loss[...])),
        ).T
        soft = jnp.exp(logits[...] - packed[:, 0:1]) / packed[:, 1:2]
        target = probs[...] / packed[:, 2:3]
        grads[...] = (packed[:, 3:4] * (soft - target)).astype(BF16)
        total[...] = jnp.zeros_like(total)

    group = mask.shape[0]
    width = mask.shape[2]
    half = group // 4
    values = grads[...]
    for at in range(0, group, half):
        gated = (mask[at : at + half] * values[None]).reshape(half * rows, width)
        query_part[0, at : at + half] = (
            jnp.dot(gated, keys[...], preferred_element_type=F32)
            .astype(BF16)
            .reshape(half, rows, keys.shape[1])
        )
        left = scaled[at : at + half].reshape(half * rows, keys.shape[1])
        total[...] += lax.dot_general(
            left, gated, (((0,), (0,)), ((), ())), preferred_element_type=F32
        )

    @pl.when(step == steps - 1)
    def _():
        key_part[...] = total[...].astype(BF16)


def gradients(place, logits, probs, stats, loss, mask, keys, scaled):
    heads, rows, width = mask.shape
    depth = keys.shape[1]
    group = heads // NX
    turn = lambda i, p: (lax.rem(p[2] + i, NX), 0, 0)
    fixed2 = lambda i, p: (0, 0)
    return pl.pallas_call(
        functools.partial(grad_kernel, steps=NX),
        grid_spec=pltpu.PrefetchScalarGridSpec(
            num_scalar_prefetch=1,
            grid=(NX,),
            in_specs=[
                pl.BlockSpec((rows, width), fixed2),
                pl.BlockSpec((rows, width), fixed2),
                pl.BlockSpec(stats.shape, lambda i, p: (0, 0, 0)),
                pl.BlockSpec((1, rows), fixed2),
                pl.BlockSpec((group, rows, width), turn),
                pl.BlockSpec((width, depth), fixed2),
                pl.BlockSpec((group, rows, depth), turn),
            ],
            out_specs=[
                pl.BlockSpec((1, group, rows, depth), lambda i, p: (i, 0, 0, 0)),
                pl.BlockSpec((depth, width), fixed2),
            ],
            scratch_shapes=[pltpu.VMEM((rows, width), BF16), pltpu.VMEM((depth, width), F32)],
        ),
        out_shape=[
            jax.ShapeDtypeStruct((NX, group, rows, depth), BF16),
            jax.ShapeDtypeStruct((depth, width), BF16),
        ],
        compiler_params=pltpu.CompilerParams(vmem_limit_bytes=40 * MIB),
        cost_estimate=pl.CostEstimate(
            flops=4 * heads * rows * depth * width, bytes_accessed=12 * MIB, transcendentals=0
        ),
        name="gradients",
    )(place, logits, probs, stats, loss, mask, keys, scaled)


def per_device(
    main_queries, main_keys, log_sums, index_queries, index_weights, index_keys, loss_weights
):
    rows, heads, depth = index_queries.shape
    width = index_keys.shape[0]
    scale = main_queries.shape[2] ** (-0.5)
    x, z = lax.axis_index("x"), lax.axis_index("z")
    place = jnp.stack([lax.axis_index("y"), lax.axis_index("core"), x]).astype(jnp.int32)

    keep, send = head_scores(
        place,
        jnp.transpose(main_queries, (1, 2, 0)),
        jnp.transpose(main_keys, (1, 2, 0)),
        log_sums.T,
        rows,
        scale,
    )
    arrived = rotate(send, "core", 1)
    pairs = [(keep[r].astype(F32) + arrived[r].astype(F32)).astype(BF16) for r in range(NY)]
    parts = [pairs[0]] + [rotate(pairs[r], "y", r) for r in range(1, NY)]

    turned = jnp.transpose(index_queries, (1, 0, 2))
    weight_columns = index_weights.T.astype(F32)[:, :, None]
    logits, mask = index_logits(turned, index_keys, weight_columns)
    scaled = (turned.astype(F32) * weight_columns).astype(BF16)

    probs, stats = local_stats(logits, parts)
    everywhere = lax.all_to_all(
        jnp.broadcast_to(stats[None], (NX * NZ, *stats.shape)),
        ("x", "z"),
        split_axis=0,
        concat_axis=0,
        tiled=True,
    )
    query_part, key_part = gradients(
        place, logits, probs, everywhere, loss_weights[None], mask, index_keys, scaled
    )
    across = [query_part[0]] + [rotate(query_part[r], "x", r) for r in range(1, NX)]
    summed = sum(part.astype(F32) for part in across).astype(BF16)
    pieces = lax.all_to_all(
        summed.reshape(NZ, heads // (NX * NZ), rows, depth),
        "z",
        split_axis=0,
        concat_axis=0,
        tiled=True,
    )
    owned = pieces.astype(F32).sum(axis=0)
    mine = heads // (NX * NZ)
    first = (x * NZ + z) * mine
    own_queries = lax.dynamic_slice_in_dim(turned, first, mine, 0).astype(F32)
    own_weights = lax.dynamic_slice_in_dim(weight_columns, first, mine, 0)
    query_grad = jnp.transpose((owned * own_weights).astype(BF16), (1, 0, 2))
    weight_grad = jnp.sum(owned * own_queries, axis=2).T

    key_pieces = lax.all_to_all(
        key_part.reshape(NY * NC, depth // (NY * NC), width),
        ("y", "core"),
        split_axis=0,
        concat_axis=0,
        tiled=True,
    )
    key_grad = key_pieces.astype(F32).sum(axis=0).astype(BF16).T
    return query_grad, weight_grad, key_grad


def solution(mesh):
    fine = Mesh(mesh.devices.reshape(NY, NC, NX, NZ), ("y", "core", "x", "z"))
    head, ctx = ("y", "core"), ("x", "z")
    return jax.shard_map(
        per_device,
        mesh=fine,
        in_specs=(
            P(None, head, None),
            P(ctx, head, None),
            P(None, head),
            P(head, None, None),
            P(head, None),
            P(ctx, None),
            P(head),
        ),
        out_specs=(P(head, ctx, None), P(head, ctx), P(ctx, head)),
        check_vma=False,
    )
```

```python
import functools
import math

import jax
import jax.numpy as jnp
from jax import lax
from jax.experimental import pallas as pl
from jax.experimental.pallas import tpu as pltpu
from jax.sharding import Mesh, PartitionSpec as P

F32 = jnp.float32
BF16 = jnp.bfloat16
NY, NC, NX, NZ = 4, 2, 4, 8
MIB = 1 << 20
LARGE = pltpu.CompilerParams(vmem_limit_bytes=60 * MIB)
SMALL = pltpu.CompilerParams(vmem_limit_bytes=12 * MIB)
HERE = pl.BlockSpec(memory_space=pltpu.VMEM)
SCALARS = pl.BlockSpec(memory_space=pltpu.SMEM)
AWAY = pl.BlockSpec(memory_space=pl.ANY)


def rotate(array, axis, shift):
    n = lax.axis_size(axis)
    return lax.ppermute(array, axis, [(i, (i + shift) % n) for i in range(n)])


def score_kernel(
    place, queries_far, keys_far, logs, keep, send, queries, keys, total, arrived, *, rows, scale
):
    heads, depth, cols = queries.shape

    def fetch(head):
        return (
            pltpu.make_async_copy(queries_far.at[head], queries.at[head], arrived.at[0, head]),
            pltpu.make_async_copy(keys_far.at[head], keys.at[head], arrived.at[1, head]),
        )

    for head in range(heads):
        for copy in fetch(head):
            copy.start()
    factor = scale * math.log2(math.e)
    ones = jnp.ones((16, keys.shape[2]), BF16)
    line = lax.broadcasted_iota(jnp.int32, (16, cols), 0)

    total[...] = jnp.zeros_like(total)

    def plain_head(head, carry):
        for copy in fetch(head):
            copy.wait()
        log_row = logs[pl.ds(head, 1), :] * (-1.0 / scale)
        high = log_row.astype(BF16).astype(F32)
        rest = log_row - high
        middle = rest.astype(BF16).astype(F32)
        low = rest - middle
        extra = jnp.where(
            line == 0, high, jnp.where(line == 1, middle, jnp.where(line == 2, low, 0.0))
        ).astype(BF16)
        left = jnp.concatenate([queries[head], extra], axis=0).T
        right = jnp.concatenate([keys[head], ones], axis=0)
        tile = 128
        for at in range(0, cols, tile):
            scores = jnp.dot(left[at : at + tile], right, preferred_element_type=F32)
            total[at : at + tile, :] += jnp.exp2(scores * factor)
        return carry

    lax.fori_loop(0, heads, plain_head, 0)
    y, core = place[0], place[1]
    for r in range(NY):
        base = lax.rem(y + r, NY) * (NC * rows)
        mine = pl.multiple_of(base + core * rows, rows)
        other = pl.multiple_of(base + (1 - core) * rows, rows)
        keep[r] = total[pl.ds(mine, rows), :].astype(BF16)
        send[r] = total[pl.ds(other, rows), :].astype(BF16)


def head_scores(place, queries, keys, logs, rows, scale):
    heads, depth, count = queries.shape
    width = keys.shape[2]
    out = jax.ShapeDtypeStruct((NY, rows, width), BF16)
    return pl.pallas_call(
        functools.partial(score_kernel, rows=rows, scale=scale),
        in_specs=[SCALARS, AWAY, AWAY, HERE],
        out_specs=[HERE, HERE],
        scratch_shapes=[
            pltpu.VMEM(queries.shape, BF16),
            pltpu.VMEM(keys.shape, BF16),
            pltpu.VMEM((count, width), F32),
            pltpu.SemaphoreType.DMA((2, heads)),
        ],
        out_shape=[out, out],
        compiler_params=LARGE,
        cost_estimate=pl.CostEstimate(
            flops=2 * heads * depth * count * width,
            bytes_accessed=12 * MIB,
            transcendentals=heads * count * width,
        ),
        name="head_scores",
    )(place, queries, keys, logs)


def column(array, index):
    lane = lax.broadcasted_iota(jnp.int32, array.shape, 1)
    return jnp.sum(jnp.where(lane == index, array, 0.0), axis=1, keepdims=True)


def logit_kernel(queries, keys, weights, expo, sums, mask, scaled, logits):
    heads, rows, depth = queries.shape
    width = keys.shape[0]
    group, tile = 8, 256
    every = weights[...].astype(F32)
    logits[...] = jnp.zeros_like(logits)

    def some_heads(step, carry):
        first = step * group
        columns = [column(every, first + k) for k in range(group)]
        here = queries[pl.ds(first, group)]
        for k in range(group):
            scaled[first + k] = (here[k].astype(F32) * columns[k]).astype(BF16)
        flat = here.reshape(group * rows, depth)
        for at in range(0, width, tile):
            raw = lax.dot_general(
                flat, keys[at : at + tile], (((1,), (1,)), ((), ())), preferred_element_type=F32
            ).reshape(group, rows, tile)
            mask[pl.ds(first, group), :, at : at + tile] = jnp.where(raw > 0, 1.0, 0.0).astype(BF16)
            added = logits[:, at : at + tile]
            for k in range(group):
                added += columns[k] * jnp.maximum(raw[k], 0.0)
            logits[:, at : at + tile] = added
        return carry

    lax.fori_loop(0, heads // group, some_heads, 0)
    values = logits[...]
    top = jnp.max(values, axis=1, keepdims=True)
    powers = jnp.exp(values - top)
    total = jnp.sum(powers, axis=1, keepdims=True)
    lane = lax.broadcasted_iota(jnp.int32, sums.shape, 1)
    expo[...] = powers
    sums[...] = jnp.where(lane == 0, top, jnp.where(lane == 1, total, 0.0))


def index_logits(queries, keys, weights):
    heads, rows, depth = queries.shape
    width = keys.shape[0]
    return pl.pallas_call(
        logit_kernel,
        in_specs=[HERE] * 3,
        out_specs=[HERE] * 4,
        out_shape=[
            jax.ShapeDtypeStruct((rows, width), F32),
            jax.ShapeDtypeStruct((rows, 128), F32),
            jax.ShapeDtypeStruct((heads, rows, width), BF16),
            jax.ShapeDtypeStruct((heads, rows, depth), BF16),
        ],
        scratch_shapes=[pltpu.VMEM((rows, width), F32)],
        compiler_params=SMALL,
        cost_estimate=pl.CostEstimate(
            flops=2 * heads * rows * depth * width,
            bytes_accessed=10 * MIB,
            transcendentals=0,
        ),
        name="index_logits",
    )(queries, keys, weights)


def stats_kernel(sums, one, two, three, four, probs, stats):
    summed = (
        one[...].astype(F32) + two[...].astype(F32) + three[...].astype(F32) + four[...].astype(F32)
    )
    probs[...] = summed
    mass = jnp.sum(summed, axis=1, keepdims=True)
    lane = lax.broadcasted_iota(jnp.int32, sums.shape, 1)
    packed = jnp.where(lane == 2, mass, sums[...])
    line = packed.T[:8]
    full = jnp.concatenate([line, jnp.zeros_like(line)], axis=1)
    stats[...] = jnp.broadcast_to(full[None], stats.shape)


def local_stats(sums, parts):
    rows, width = parts[0].shape
    return pl.pallas_call(
        stats_kernel,
        out_shape=[
            jax.ShapeDtypeStruct((rows, width), F32),
            jax.ShapeDtypeStruct((NX * NZ, 8, 2 * rows), F32),
        ],
        in_specs=[HERE] * (1 + len(parts)),
        out_specs=[HERE, HERE],
        compiler_params=SMALL,
        name="local_stats",
    )(sums, *parts)


def query_terms(mask, first, keys, values, out):
    count, rows, depth = out.shape
    width = keys.shape[0]
    half = count // 2
    for at in range(0, count, half):
        gated = (mask[pl.ds(first + at, half)] * values[None]).reshape(half * rows, width)
        term = jnp.dot(gated, keys[...], preferred_element_type=F32)
        out[at : at + half] = term.astype(BF16).reshape(half, rows, depth)


def far_kernel(place, expo, sums, probs, stats, loss, mask, keys, grads, one, two, three):
    rows = expo.shape[0]
    each = stats[...]
    tops = each[:, 0, :]
    top = jnp.max(tops, axis=0, keepdims=True)
    denominator = jnp.sum(each[:, 1, :] * jnp.exp(tops - top), axis=0, keepdims=True)
    mass = jnp.sum(each[:, 2, :], axis=0, keepdims=True)
    line = lax.broadcasted_iota(jnp.int32, (128, 2 * rows), 0)
    packed = jnp.where(line == 0, top, jnp.where(line == 1, denominator, mass)).T[:rows]
    weight = jnp.broadcast_to(loss[...], (128, rows)).T[:, 0:1]
    soft = expo[...] * (jnp.exp(sums[:, 0:1] - packed[:, 0:1]) / packed[:, 1:2])
    target = probs[...] / packed[:, 2:3]
    values = (weight * (soft - target)).astype(BF16)
    grads[...] = values
    for r, out in ((1, one), (2, two), (3, three)):
        first = lax.rem(place[2] + r, NX) * out.shape[0]
        query_terms(mask, first, keys, values, out)


def far_terms(place, expo, sums, probs, stats, loss, mask, keys):
    heads, rows, width = mask.shape
    depth = keys.shape[1]
    part = jax.ShapeDtypeStruct((heads // NX, rows, depth), BF16)
    return pl.pallas_call(
        far_kernel,
        in_specs=[SCALARS] + [HERE] * 7,
        out_specs=[HERE] * 4,
        out_shape=[jax.ShapeDtypeStruct((rows, width), BF16), part, part, part],
        compiler_params=SMALL,
        cost_estimate=pl.CostEstimate(
            flops=heads * rows * depth * width, bytes_accessed=8 * MIB, transcendentals=0
        ),
        name="far_terms",
    )(place, expo, sums, probs, stats, loss, mask, keys)


def near_kernel(place, grads, mask, keys, scaled, own, key_part, total):
    heads, rows, width = mask.shape
    depth = keys.shape[1]
    values = grads[...]
    query_terms(mask, place[2] * own.shape[0], keys, values, own)
    group = 8
    total[...] = jnp.zeros_like(total)

    def some_heads(step, carry):
        first = step * group
        gated = (mask[pl.ds(first, group)] * values[None]).reshape(group * rows, width)
        left = scaled[pl.ds(first, group)].reshape(group * rows, depth)
        total[...] += lax.dot_general(
            left, gated, (((0,), (0,)), ((), ())), preferred_element_type=F32
        )
        return carry

    lax.fori_loop(0, heads // group, some_heads, 0)
    key_part[...] = total[...].astype(BF16)


def near_terms(place, grads, mask, keys, scaled):
    heads, rows, width = mask.shape
    depth = keys.shape[1]
    return pl.pallas_call(
        near_kernel,
        in_specs=[SCALARS] + [HERE] * 4,
        out_specs=[HERE] * 2,
        scratch_shapes=[pltpu.VMEM((depth, width), F32)],
        out_shape=[
            jax.ShapeDtypeStruct((heads // NX, rows, depth), BF16),
            jax.ShapeDtypeStruct((depth, width), BF16),
        ],
        compiler_params=SMALL,
        cost_estimate=pl.CostEstimate(
            flops=3 * heads * rows * depth * width, bytes_accessed=10 * MIB, transcendentals=0
        ),
        name="near_terms",
    )(place, grads, mask, keys, scaled)


def last_kernel(place, pieces, queries, weights, query_grad, weight_grad):
    summed = pieces[0].astype(F32)
    for k in range(1, pieces.shape[0]):
        summed += pieces[k].astype(F32)
    mine = pieces.shape[1]
    every = weights[...].astype(F32)
    for k in range(mine):
        dots = jnp.sum(summed[k] * queries[k].astype(F32), axis=1, keepdims=True)
        weight_grad[k : k + 1, :] = jnp.broadcast_to(dots, (dots.shape[0], 128)).T[0:1]
        query_grad[:, k, :] = (summed[k] * column(every, place[3] * mine + k)).astype(BF16)


def last_sums(place, pieces, queries, weights):
    count, mine, rows, depth = pieces.shape
    return pl.pallas_call(
        last_kernel,
        grid_spec=pltpu.PrefetchScalarGridSpec(
            num_scalar_prefetch=1,
            grid=(1,),
            in_specs=[
                pl.BlockSpec(pieces.shape, lambda i, p: (0, 0, 0, 0)),
                pl.BlockSpec((mine, rows, depth), lambda i, p: (p[3], 0, 0)),
                pl.BlockSpec(weights.shape, lambda i, p: (0, 0)),
            ],
            out_specs=[
                pl.BlockSpec((rows, mine, depth), lambda i, p: (0, 0, 0)),
                pl.BlockSpec((mine, rows), lambda i, p: (0, 0)),
            ],
        ),
        out_shape=[
            jax.ShapeDtypeStruct((rows, mine, depth), BF16),
            jax.ShapeDtypeStruct((mine, rows), F32),
        ],
        compiler_params=SMALL,
        name="last_sums",
    )(place, pieces, queries, weights)


def per_device(
    main_queries, main_keys, log_sums, index_queries, index_weights, index_keys, loss_weights
):
    rows, heads, depth = index_queries.shape
    width = index_keys.shape[0]
    scale = main_queries.shape[2] ** (-0.5)
    x, z = lax.axis_index("x"), lax.axis_index("z")
    place = jnp.stack([lax.axis_index("y"), lax.axis_index("core"), x, x * NZ + z])

    keep, send = head_scores(
        place,
        jnp.transpose(main_queries, (1, 2, 0)),
        jnp.transpose(main_keys, (1, 2, 0)),
        log_sums.T,
        rows,
        scale,
    )
    arrived = rotate(send, "core", 1)
    pairs = [(keep[r].astype(F32) + arrived[r].astype(F32)).astype(BF16) for r in range(NY)]
    parts = [pairs[0]] + [rotate(pairs[r], "y", r) for r in range(1, NY)]

    turned = jnp.transpose(index_queries, (1, 0, 2))
    expo, sums, mask, scaled = index_logits(turned, index_keys, index_weights)

    probs, stats = local_stats(sums, parts)
    everywhere = lax.all_to_all(stats, ("x", "z"), split_axis=0, concat_axis=0, tiled=True)
    grads, one, two, three = far_terms(
        place, expo, sums, probs, everywhere, loss_weights[None], mask, index_keys
    )
    across = [rotate(term, "x", r) for r, term in ((1, one), (2, two), (3, three))]
    own, key_part = near_terms(place, grads, mask, index_keys, scaled)
    summed = sum(part.astype(F32) for part in [own] + across).astype(BF16)
    pieces = lax.all_to_all(
        summed.reshape(NZ, heads // (NX * NZ), rows, depth),
        "z",
        split_axis=0,
        concat_axis=0,
        tiled=True,
    )
    query_grad, weight_grad = last_sums(place, pieces, turned, index_weights)

    key_pieces = lax.all_to_all(
        key_part.reshape(NY * NC, depth // (NY * NC), width),
        ("y", "core"),
        split_axis=0,
        concat_axis=0,
        tiled=True,
    )
    key_grad = key_pieces.astype(F32).sum(axis=0).astype(BF16).T
    return query_grad, weight_grad.T, key_grad


def solution(mesh):
    fine = Mesh(mesh.devices.reshape(NY, NC, NX, NZ), ("y", "core", "x", "z"))
    head, ctx = ("y", "core"), ("x", "z")
    return jax.shard_map(
        per_device,
        mesh=fine,
        in_specs=(
            P(None, head, None),
            P(ctx, head, None),
            P(None, head),
            P(head, None, None),
            P(head, None),
            P(ctx, None),
            P(head),
        ),
        out_specs=(P(head, ctx, None), P(head, ctx), P(ctx, head)),
        check_vma=False,
    )
```

```python
import functools
import math

import jax
import jax.numpy as jnp
from jax import lax
from jax.experimental import pallas as pl
from jax.experimental.pallas import tpu as pltpu
from jax.sharding import Mesh, PartitionSpec as P

F32 = jnp.float32
BF16 = jnp.bfloat16
NY, NC, NX, NZ = 4, 2, 4, 8
MIB = 1 << 20
LARGE = pltpu.CompilerParams(vmem_limit_bytes=50 * MIB)
SMALL = pltpu.CompilerParams(vmem_limit_bytes=12 * MIB)
HERE = pl.BlockSpec(memory_space=pltpu.VMEM)
AWAY = pl.BlockSpec(memory_space=pl.ANY)


def rotate(array, axis, shift):
    n = lax.axis_size(axis)
    return lax.ppermute(array, axis, [(i, (i + shift) % n) for i in range(n)])


def score_kernel(
    queries_far, keys_far, logs, keep, send, queries, keys, total, arrived, *, rows, scale
):
    heads, depth, cols = queries.shape

    def fetch(head):
        return (
            pltpu.make_async_copy(queries_far.at[head], queries.at[head], arrived.at[0, head]),
            pltpu.make_async_copy(keys_far.at[head], keys.at[head], arrived.at[1, head]),
        )

    for head in range(heads):
        for copy in fetch(head):
            copy.start()
    factor = scale * math.log2(math.e)
    ones = jnp.ones((16, keys.shape[2]), BF16)
    line = lax.broadcasted_iota(jnp.int32, (16, cols), 0)

    tile = 256
    total[...] = jnp.zeros_like(total)

    def operands(head):
        log_row = logs[pl.ds(head, 1), :] * (-1.0 / scale)
        high = log_row.astype(BF16).astype(F32)
        rest = log_row - high
        middle = rest.astype(BF16).astype(F32)
        low = rest - middle
        extra = jnp.where(
            line == 0, high, jnp.where(line == 1, middle, jnp.where(line == 2, low, 0.0))
        ).astype(BF16)
        left = jnp.concatenate([queries[head], extra], axis=0).T
        return left, jnp.concatenate([keys[head], ones], axis=0)

    group = 4

    def some_heads(step, carry):
        first = step * group
        for k in range(group):
            for copy in fetch(first + k):
                copy.wait()
        pairs = [operands(first + k) for k in range(group)]

        for k in range(group):
            left, right = pairs[k]
            for at in range(0, cols, tile):
                scores = jnp.dot(left[at : at + tile], right, preferred_element_type=F32)
                total[at : at + tile, :] += jnp.exp2(scores * factor)
        return carry

    lax.fori_loop(0, heads // group, some_heads, 0)
    y, core = lax.axis_index("y"), lax.axis_index("core")
    for r in range(NY):
        base = lax.rem(y + r, NY) * (NC * rows)
        mine = pl.multiple_of(base + core * rows, rows)
        other = pl.multiple_of(base + (1 - core) * rows, rows)
        keep[r] = total[pl.ds(mine, rows), :].astype(BF16)
        send[r] = total[pl.ds(other, rows), :].astype(BF16)


def head_scores(queries, keys, logs, rows, scale):
    heads, depth, count = queries.shape
    width = keys.shape[2]
    out = jax.ShapeDtypeStruct((NY, rows, width), BF16)
    return pl.pallas_call(
        functools.partial(score_kernel, rows=rows, scale=scale),
        in_specs=[AWAY, AWAY, HERE],
        out_specs=[HERE, HERE],
        scratch_shapes=[
            pltpu.VMEM(queries.shape, BF16),
            pltpu.VMEM(keys.shape, BF16),
            pltpu.VMEM((count, width), F32),
            pltpu.SemaphoreType.DMA((2, heads)),
        ],
        out_shape=[out, out],
        compiler_params=LARGE,
        cost_estimate=pl.CostEstimate(
            flops=2 * heads * depth * count * width,
            bytes_accessed=12 * MIB,
            transcendentals=heads * count * width,
        ),
        name="head_scores",
    )(queries, keys, logs)


def column(array, index):
    lane = lax.broadcasted_iota(jnp.int32, array.shape, 1)
    return jnp.sum(jnp.where(lane == index, array, 0.0), axis=1, keepdims=True)


def logit_kernel(queries, keys, weights, expo, sums, mask, scaled, logits):
    heads, rows, depth = queries.shape
    width = keys.shape[0]
    group, tile = 8, 256
    every = weights[...].astype(F32)
    logits[...] = jnp.zeros_like(logits)

    def some_heads(step, carry):
        first = step * group
        columns = [column(every, first + k) for k in range(group)]
        here = queries[pl.ds(first, group)]
        for k in range(group):
            scaled[first + k] = (here[k].astype(F32) * columns[k]).astype(BF16)
        flat = here.reshape(group * rows, depth)
        for at in range(0, width, tile):
            raw = lax.dot_general(
                flat, keys[at : at + tile], (((1,), (1,)), ((), ())), preferred_element_type=F32
            ).reshape(group, rows, tile)
            mask[pl.ds(first, group), :, at : at + tile] = jnp.where(raw > 0, 1.0, 0.0).astype(BF16)
            added = logits[:, at : at + tile]
            for k in range(group):
                added += columns[k] * jnp.maximum(raw[k], 0.0)
            logits[:, at : at + tile] = added
        return carry

    lax.fori_loop(0, heads // group, some_heads, 0)
    values = logits[...]
    top = jnp.max(values, axis=1, keepdims=True)
    powers = jnp.exp(values - top)
    total = jnp.sum(powers, axis=1, keepdims=True)
    lane = lax.broadcasted_iota(jnp.int32, sums.shape, 1)
    expo[...] = powers
    sums[...] = jnp.where(lane == 0, top, jnp.where(lane == 1, total, 0.0))


def index_logits(queries, keys, weights):
    heads, rows, depth = queries.shape
    width = keys.shape[0]
    return pl.pallas_call(
        logit_kernel,
        in_specs=[HERE] * 3,
        out_specs=[HERE] * 4,
        out_shape=[
            jax.ShapeDtypeStruct((rows, width), F32),
            jax.ShapeDtypeStruct((rows, 128), F32),
            jax.ShapeDtypeStruct((heads, rows, width), BF16),
            jax.ShapeDtypeStruct((heads, rows, depth), BF16),
        ],
        scratch_shapes=[pltpu.VMEM((rows, width), F32)],
        compiler_params=SMALL,
        cost_estimate=pl.CostEstimate(
            flops=2 * heads * rows * depth * width,
            bytes_accessed=10 * MIB,
            transcendentals=0,
        ),
        name="index_logits",
    )(queries, keys, weights)


def stats_kernel(sums, one, two, three, four, probs, stats):
    summed = (
        one[...].astype(F32) + two[...].astype(F32) + three[...].astype(F32) + four[...].astype(F32)
    )
    probs[...] = summed
    mass = jnp.sum(summed, axis=1, keepdims=True)
    lane = lax.broadcasted_iota(jnp.int32, sums.shape, 1)
    packed = jnp.where(lane == 2, mass, sums[...])
    line = packed.T[:8]
    full = jnp.concatenate([line, jnp.zeros_like(line)], axis=1)
    stats[...] = jnp.broadcast_to(full[None], stats.shape)


def local_stats(sums, parts):
    rows, width = parts[0].shape
    return pl.pallas_call(
        stats_kernel,
        out_shape=[
            jax.ShapeDtypeStruct((rows, width), F32),
            jax.ShapeDtypeStruct((NX * NZ, 8, 2 * rows), F32),
        ],
        in_specs=[HERE] * (1 + len(parts)),
        out_specs=[HERE, HERE],
        compiler_params=SMALL,
        name="local_stats",
    )(sums, *parts)


def query_terms(mask, first, keys, values, out):
    count, rows, depth = out.shape
    width = keys.shape[0]
    half = count // 2
    for at in range(0, count, half):
        gated = (mask[pl.ds(first + at, half)] * values[None]).reshape(half * rows, width)
        term = jnp.dot(gated, keys[...], preferred_element_type=F32)
        out[at : at + half] = term.astype(BF16).reshape(half, rows, depth)


def far_kernel(expo, sums, probs, stats, loss, mask, keys, grads, one, two, three):
    rows = expo.shape[0]
    each = stats[...]
    tops = each[:, 0, :]
    top = jnp.max(tops, axis=0, keepdims=True)
    denominator = jnp.sum(each[:, 1, :] * jnp.exp(tops - top), axis=0, keepdims=True)
    mass = jnp.sum(each[:, 2, :], axis=0, keepdims=True)
    line = lax.broadcasted_iota(jnp.int32, (128, 2 * rows), 0)
    packed = jnp.where(line == 0, top, jnp.where(line == 1, denominator, mass)).T[:rows]
    weight = jnp.broadcast_to(loss[...], (128, rows)).T[:, 0:1]
    soft = expo[...] * (jnp.exp(sums[:, 0:1] - packed[:, 0:1]) / packed[:, 1:2])
    target = probs[...] / packed[:, 2:3]
    values = (weight * (soft - target)).astype(BF16)
    grads[...] = values
    for r, out in ((1, one), (2, two), (3, three)):
        first = lax.rem(lax.axis_index("x") + r, NX) * out.shape[0]
        query_terms(mask, first, keys, values, out)


def far_terms(expo, sums, probs, stats, loss, mask, keys):
    heads, rows, width = mask.shape
    depth = keys.shape[1]
    part = jax.ShapeDtypeStruct((heads // NX, rows, depth), BF16)
    return pl.pallas_call(
        far_kernel,
        in_specs=[HERE] * 7,
        out_specs=[HERE] * 4,
        out_shape=[jax.ShapeDtypeStruct((rows, width), BF16), part, part, part],
        compiler_params=SMALL,
        cost_estimate=pl.CostEstimate(
            flops=heads * rows * depth * width, bytes_accessed=8 * MIB, transcendentals=0
        ),
        name="far_terms",
    )(expo, sums, probs, stats, loss, mask, keys)


def own_kernel(grads, mask, keys, own):
    query_terms(mask, lax.axis_index("x") * own.shape[0], keys, grads[...], own)


def own_terms(grads, mask, keys):
    heads, rows, width = mask.shape
    depth = keys.shape[1]
    return pl.pallas_call(
        own_kernel,
        in_specs=[HERE] * 3,
        out_specs=HERE,
        out_shape=jax.ShapeDtypeStruct((heads // NX, rows, depth), BF16),
        compiler_params=SMALL,
        cost_estimate=pl.CostEstimate(
            flops=heads * rows * depth * width // 2, bytes_accessed=2 * MIB, transcendentals=0
        ),
        name="own_terms",
    )(grads, mask, keys)


def key_kernel(grads, mask, scaled, keep, send, total):
    heads, rows, width = mask.shape
    depth = scaled.shape[2]
    values = grads[...]
    group = 8
    total[...] = jnp.zeros_like(total)

    def some_heads(step, carry):
        first = step * group
        gated = (mask[pl.ds(first, group)] * values[None]).reshape(group * rows, width)
        left = scaled[pl.ds(first, group)].reshape(group * rows, depth)
        total[...] += lax.dot_general(
            left, gated, (((0,), (0,)), ((), ())), preferred_element_type=F32
        )
        return carry

    lax.fori_loop(0, heads // group, some_heads, 0)
    y, core = lax.axis_index("y"), lax.axis_index("core")
    count = keep.shape[1]
    for r in range(NY):
        base = lax.rem(y + r, NY) * (NC * count)
        mine = pl.multiple_of(base + core * count, count)
        other = pl.multiple_of(base + (1 - core) * count, count)
        keep[r] = total[pl.ds(mine, count), :].astype(BF16)
        send[r] = total[pl.ds(other, count), :].astype(BF16)


def key_terms(grads, mask, scaled):
    heads, rows, width = mask.shape
    depth = scaled.shape[2]
    out = jax.ShapeDtypeStruct((NY, depth // (NY * NC), width), BF16)
    return pl.pallas_call(
        key_kernel,
        in_specs=[HERE] * 3,
        out_specs=[HERE] * 2,
        out_shape=[out, out],
        scratch_shapes=[pltpu.VMEM((depth, width), F32)],
        compiler_params=SMALL,
        cost_estimate=pl.CostEstimate(
            flops=2 * heads * rows * depth * width, bytes_accessed=10 * MIB, transcendentals=0
        ),
        name="key_terms",
    )(grads, mask, scaled)


def last_kernel(pieces, queries, weights, query_grad, weight_grad):
    summed = pieces[0].astype(F32)
    for k in range(1, pieces.shape[0]):
        summed += pieces[k].astype(F32)
    mine = pieces.shape[1]
    first = (lax.axis_index("x") * NZ + lax.axis_index("z")) * mine
    every = weights[...].astype(F32)
    for k in range(mine):
        own = queries[first + k].astype(F32)
        dots = jnp.sum(summed[k] * own, axis=1, keepdims=True)
        weight_grad[k : k + 1, :] = jnp.broadcast_to(dots, (dots.shape[0], 128)).T[0:1]
        query_grad[:, k, :] = (summed[k] * column(every, first + k)).astype(BF16)


def last_sums(pieces, queries, weights):
    count, mine, rows, depth = pieces.shape
    return pl.pallas_call(
        last_kernel,
        in_specs=[HERE] * 3,
        out_specs=[HERE] * 2,
        out_shape=[
            jax.ShapeDtypeStruct((rows, mine, depth), BF16),
            jax.ShapeDtypeStruct((mine, rows), F32),
        ],
        compiler_params=SMALL,
        name="last_sums",
    )(pieces, queries, weights)


def sum_kernel(*refs, count):
    total = refs[0][...].astype(F32)
    for part in refs[1:count]:
        total += part[...].astype(F32)
    refs[-1][...] = total.astype(BF16)


def sum_parts(parts, name, after=()):
    return pl.pallas_call(
        functools.partial(sum_kernel, count=len(parts)),
        in_specs=[HERE] * (len(parts) + len(after)),
        out_specs=HERE,
        out_shape=jax.ShapeDtypeStruct(parts[0].shape, BF16),
        compiler_params=SMALL,
        name=name,
    )(*parts, *after)


def pair_kernel(keep, arrived, *outs):
    for r, out in enumerate(outs):
        out[...] = (keep[r].astype(F32) + arrived[r].astype(F32)).astype(BF16)


def sum_pair(keep, arrived, name):
    part = jax.ShapeDtypeStruct(keep.shape[1:], BF16)
    return pl.pallas_call(
        pair_kernel,
        in_specs=[HERE] * 2,
        out_specs=[HERE] * NY,
        out_shape=[part] * NY,
        compiler_params=SMALL,
        name=name,
    )(keep, arrived)


def sum_over_heads(keep, send, name):
    with jax.named_scope(name + "_core"):
        arrived = rotate(send, "core", 1)
    pairs = sum_pair(keep, arrived, name)
    with jax.named_scope(name + "_y"):
        return [pairs[0]] + [rotate(pairs[r], "y", r) for r in (2, 1, 3)]


def per_device(
    main_queries, main_keys, log_sums, index_queries, index_weights, index_keys, loss_weights
):
    rows, heads, depth = index_queries.shape
    width = index_keys.shape[0]
    scale = main_queries.shape[2] ** (-0.5)
    keep, send = head_scores(
        jnp.transpose(main_queries, (1, 2, 0)),
        jnp.transpose(main_keys, (1, 2, 0)),
        log_sums.T,
        rows,
        scale,
    )
    parts = sum_over_heads(keep, send, "pair_probs")

    turned = jnp.transpose(index_queries, (1, 0, 2))
    expo, sums, mask, scaled = index_logits(turned, index_keys, index_weights)

    probs, stats = local_stats(sums, parts)
    everywhere = lax.all_to_all(stats, ("x", "z"), split_axis=0, concat_axis=0, tiled=True)
    grads, one, two, three = far_terms(
        expo, sums, probs, everywhere, loss_weights[None], mask, index_keys
    )
    with jax.named_scope("x_turns"):
        across = [rotate(term, "x", r) for r, term in ((2, two), (1, one), (3, three))]
    key_keep, key_send = key_terms(grads, mask, scaled)
    key_parts = sum_over_heads(key_keep, key_send, "pair_keys")
    own = own_terms(grads, mask, index_keys)
    summed = sum_parts([own] + across, "x_sums", key_parts[:1])
    with jax.named_scope("z_exchange"):
        pieces = lax.all_to_all(
            summed.reshape(NZ, heads // (NX * NZ), rows, depth),
            "z",
            split_axis=0,
            concat_axis=0,
            tiled=True,
        )
    query_grad, weight_grad = last_sums(pieces, turned, index_weights)
    key_grad = sum_parts(key_parts, "key_sums")
    return query_grad, weight_grad.T, key_grad.T


def solution(mesh):
    fine = Mesh(mesh.devices.reshape(NY, NC, NX, NZ), ("y", "core", "x", "z"))
    head, ctx = ("y", "core"), ("x", "z")
    return jax.shard_map(
        per_device,
        mesh=fine,
        in_specs=(
            P(None, head, None),
            P(ctx, head, None),
            P(None, head),
            P(head, None, None),
            P(head, None),
            P(ctx, None),
            P(head),
        ),
        out_specs=(P(head, ctx, None), P(head, ctx), P(ctx, head)),
        check_vma=False,
    )
```

```python
import functools
import math

import jax
import jax.numpy as jnp
from jax import lax
from jax.experimental import pallas as pl
from jax.experimental.pallas import tpu as pltpu
from jax.sharding import Mesh, PartitionSpec as P

F32 = jnp.float32
BF16 = jnp.bfloat16
NY, NC, NX, NZ = 4, 2, 4, 8
MIB = 1 << 20
LARGE = pltpu.CompilerParams(vmem_limit_bytes=50 * MIB)
SMALL = pltpu.CompilerParams(vmem_limit_bytes=12 * MIB)
HERE = pl.BlockSpec(memory_space=pltpu.VMEM)
AWAY = pl.BlockSpec(memory_space=pl.ANY)


def rotate(array, axis, shift):
    n = lax.axis_size(axis)
    return lax.ppermute(array, axis, [(i, (i + shift) % n) for i in range(n)])


def score_kernel(
    queries_far, keys_far, logs, keep, send, queries, keys, total, arrived, *, rows, scale
):
    heads, _, cols = queries.shape

    def fetch(head):
        return (
            pltpu.make_async_copy(queries_far.at[head], queries.at[head], arrived.at[0, head]),
            pltpu.make_async_copy(keys_far.at[head], keys.at[head], arrived.at[1, head]),
        )

    for head in range(heads):
        for copy in fetch(head):
            copy.start()
    factor = scale * math.log2(math.e)
    ones = jnp.ones((16, keys.shape[2]), BF16)
    line = lax.broadcasted_iota(jnp.int32, (16, cols), 0)

    tile = 256
    total[...] = jnp.zeros_like(total)

    def operands(head):
        log_row = logs[pl.ds(head, 1), :] * (-1.0 / scale)
        high = log_row.astype(BF16).astype(F32)
        rest = log_row - high
        middle = rest.astype(BF16).astype(F32)
        low = rest - middle
        extra = jnp.where(
            line == 0, high, jnp.where(line == 1, middle, jnp.where(line == 2, low, 0.0))
        ).astype(BF16)
        left = jnp.concatenate([queries[head], extra], axis=0).T
        return left, jnp.concatenate([keys[head], ones], axis=0)

    def some_heads(first, group):
        for k in range(group):
            for copy in fetch(first + k):
                copy.wait()
        pairs = [operands(first + k) for k in range(group)]

        for k in range(group):
            left, right = pairs[k]
            for at in range(0, cols, tile):
                scores = jnp.dot(left[at : at + tile], right, preferred_element_type=F32)
                total[at : at + tile, :] += jnp.exp2(scores * factor)

    def four_heads(step, carry):
        some_heads(4 * step, 4)
        return carry

    some_heads(0, 1)
    some_heads(1, 3)
    lax.fori_loop(1, heads // 4, four_heads, 0)
    y, core = lax.axis_index("y"), lax.axis_index("core")
    for r in range(NY):
        base = lax.rem(y + r, NY) * (NC * rows)
        mine = pl.multiple_of(base + core * rows, rows)
        other = pl.multiple_of(base + (1 - core) * rows, rows)
        keep[r] = total[pl.ds(mine, rows), :].astype(BF16)
        send[r] = total[pl.ds(other, rows), :].astype(BF16)


def head_scores(queries, keys, logs, rows, scale):
    heads, depth, count = queries.shape
    width = keys.shape[2]
    out = jax.ShapeDtypeStruct((NY, rows, width), BF16)
    return pl.pallas_call(
        functools.partial(score_kernel, rows=rows, scale=scale),
        in_specs=[AWAY, AWAY, HERE],
        out_specs=[HERE, HERE],
        scratch_shapes=[
            pltpu.VMEM(queries.shape, BF16),
            pltpu.VMEM(keys.shape, BF16),
            pltpu.VMEM((count, width), F32),
            pltpu.SemaphoreType.DMA((2, heads)),
        ],
        out_shape=[out, out],
        compiler_params=LARGE,
        cost_estimate=pl.CostEstimate(
            flops=2 * heads * depth * count * width,
            bytes_accessed=12 * MIB,
            transcendentals=heads * count * width,
        ),
        name="head_scores",
    )(queries, keys, logs)


def column(array, index):
    lane = lax.broadcasted_iota(jnp.int32, array.shape, 1)
    return jnp.sum(jnp.where(lane == index, array, 0.0), axis=1, keepdims=True)


def logit_kernel(queries, keys, weights, expo, sums, mask, scaled, logits):
    heads, rows, depth = queries.shape
    width = keys.shape[0]
    group, tile = 8, 256
    every = weights[...].astype(F32)
    logits[...] = jnp.zeros_like(logits)

    def some_heads(step, carry):
        first = step * group
        columns = [column(every, first + k) for k in range(group)]
        here = queries[pl.ds(first, group)]
        for k in range(group):
            scaled[first + k] = (here[k].astype(F32) * columns[k]).astype(BF16)
        flat = here.reshape(group * rows, depth)
        for at in range(0, width, tile):
            raw = lax.dot_general(
                flat, keys[at : at + tile], (((1,), (1,)), ((), ())), preferred_element_type=F32
            ).reshape(group, rows, tile)
            mask[pl.ds(first, group), :, at : at + tile] = jnp.where(raw > 0, 1.0, 0.0).astype(BF16)
            added = logits[:, at : at + tile]
            for k in range(group):
                added += columns[k] * jnp.maximum(raw[k], 0.0)
            logits[:, at : at + tile] = added
        return carry

    lax.fori_loop(0, heads // group, some_heads, 0)
    values = logits[...]
    top = jnp.max(values, axis=1, keepdims=True)
    powers = jnp.exp(values - top)
    total = jnp.sum(powers, axis=1, keepdims=True)
    lane = lax.broadcasted_iota(jnp.int32, sums.shape, 1)
    expo[...] = powers
    sums[...] = jnp.where(lane == 0, top, jnp.where(lane == 1, total, 0.0))


def index_logits(queries, keys, weights):
    heads, rows, depth = queries.shape
    width = keys.shape[0]
    return pl.pallas_call(
        logit_kernel,
        in_specs=[HERE] * 3,
        out_specs=[HERE] * 4,
        out_shape=[
            jax.ShapeDtypeStruct((rows, width), F32),
            jax.ShapeDtypeStruct((rows, 128), F32),
            jax.ShapeDtypeStruct((heads, rows, width), BF16),
            jax.ShapeDtypeStruct((heads, rows, depth), BF16),
        ],
        scratch_shapes=[pltpu.VMEM((rows, width), F32)],
        compiler_params=SMALL,
        cost_estimate=pl.CostEstimate(
            flops=2 * heads * rows * depth * width,
            bytes_accessed=10 * MIB,
            transcendentals=0,
        ),
        name="index_logits",
    )(queries, keys, weights)


def stats_kernel(sums, one, two, three, four, probs, stats):
    summed = (
        one[...].astype(F32) + two[...].astype(F32) + three[...].astype(F32) + four[...].astype(F32)
    )
    probs[...] = summed
    mass = jnp.sum(summed, axis=1, keepdims=True)
    lane = lax.broadcasted_iota(jnp.int32, sums.shape, 1)
    packed = jnp.where(lane == 2, mass, sums[...])
    line = packed.T[:8]
    full = jnp.concatenate([line, jnp.zeros_like(line)], axis=1)
    stats[...] = jnp.broadcast_to(full[None], stats.shape)


def local_stats(sums, parts):
    rows, width = parts[0].shape
    return pl.pallas_call(
        stats_kernel,
        out_shape=[
            jax.ShapeDtypeStruct((rows, width), F32),
            jax.ShapeDtypeStruct((NX * NZ, 8, 2 * rows), F32),
        ],
        in_specs=[HERE] * (1 + len(parts)),
        out_specs=[HERE, HERE],
        compiler_params=SMALL,
        name="local_stats",
    )(sums, *parts)


def query_terms(mask, first, keys, values, out):
    count, rows, depth = out.shape
    width = keys.shape[0]
    half = count // 2
    for at in range(0, count, half):
        gated = (mask[pl.ds(first + at, half)] * values[None]).reshape(half * rows, width)
        term = jnp.dot(gated, keys[...], preferred_element_type=F32)
        out[at : at + half] = term.astype(BF16).reshape(half, rows, depth)


def far_kernel(expo, sums, probs, stats, loss, mask, keys, grads, out, *, shift):
    rows = expo.shape[0]
    each = stats[...]
    tops = each[:, 0, :]
    top = jnp.max(tops, axis=0, keepdims=True)
    denominator = jnp.sum(each[:, 1, :] * jnp.exp(tops - top), axis=0, keepdims=True)
    mass = jnp.sum(each[:, 2, :], axis=0, keepdims=True)
    line = lax.broadcasted_iota(jnp.int32, (128, 2 * rows), 0)
    packed = jnp.where(line == 0, top, jnp.where(line == 1, denominator, mass)).T[:rows]
    weight = jnp.broadcast_to(loss[...], (128, rows)).T[:, 0:1]
    soft = expo[...] * (jnp.exp(sums[:, 0:1] - packed[:, 0:1]) / packed[:, 1:2])
    target = probs[...] / packed[:, 2:3]
    values = (weight * (soft - target)).astype(BF16)
    grads[...] = values
    first = lax.rem(lax.axis_index("x") + shift, NX) * out.shape[0]
    query_terms(mask, first, keys, values, out)


def first_terms(expo, sums, probs, stats, loss, mask, keys, shift):
    heads, rows, width = mask.shape
    depth = keys.shape[1]
    part = jax.ShapeDtypeStruct((heads // NX, rows, depth), BF16)
    return pl.pallas_call(
        functools.partial(far_kernel, shift=shift),
        in_specs=[HERE] * 7,
        out_specs=[HERE] * 2,
        out_shape=[jax.ShapeDtypeStruct((rows, width), BF16), part],
        compiler_params=SMALL,
        cost_estimate=pl.CostEstimate(
            flops=heads * rows * depth * width, bytes_accessed=8 * MIB, transcendentals=0
        ),
        name="first_terms",
    )(expo, sums, probs, stats, loss, mask, keys)


def shift_kernel(grads, mask, keys, *rest, shift):
    out = rest[-1]
    first = lax.rem(lax.axis_index("x") + shift, NX) * out.shape[0]
    query_terms(mask, first, keys, grads[...], out)


def shift_terms(grads, mask, keys, shift, after=()):
    heads, rows, width = mask.shape
    depth = keys.shape[1]
    return pl.pallas_call(
        functools.partial(shift_kernel, shift=shift),
        in_specs=[HERE] * (3 + len(after)),
        out_specs=HERE,
        out_shape=jax.ShapeDtypeStruct((heads // NX, rows, depth), BF16),
        compiler_params=SMALL,
        cost_estimate=pl.CostEstimate(
            flops=heads * rows * depth * width // 2, bytes_accessed=2 * MIB, transcendentals=0
        ),
    )(grads, mask, keys, *after)


def key_kernel(grads, mask, scaled, after, keep, send, total):
    heads, rows, width = mask.shape
    depth = scaled.shape[2]
    values = grads[...]
    group = 8
    total[...] = jnp.zeros_like(total)

    def some_heads(step, carry):
        first = step * group
        gated = (mask[pl.ds(first, group)] * values[None]).reshape(group * rows, width)
        left = scaled[pl.ds(first, group)].reshape(group * rows, depth)
        total[...] += lax.dot_general(
            left, gated, (((0,), (0,)), ((), ())), preferred_element_type=F32
        )
        return carry

    lax.fori_loop(0, heads // group, some_heads, 0)
    y, core = lax.axis_index("y"), lax.axis_index("core")
    count = keep.shape[1]
    for r in range(NY):
        base = lax.rem(y + r, NY) * (NC * count)
        mine = pl.multiple_of(base + core * count, count)
        other = pl.multiple_of(base + (1 - core) * count, count)
        keep[r] = total[pl.ds(mine, count), :].astype(BF16)
        send[r] = total[pl.ds(other, count), :].astype(BF16)


def key_terms(grads, mask, scaled, after):
    heads, rows, width = mask.shape
    depth = scaled.shape[2]
    out = jax.ShapeDtypeStruct((NY, depth // (NY * NC), width), BF16)
    return pl.pallas_call(
        key_kernel,
        in_specs=[HERE] * 4,
        out_specs=[HERE] * 2,
        out_shape=[out, out],
        scratch_shapes=[pltpu.VMEM((depth, width), F32)],
        compiler_params=SMALL,
        cost_estimate=pl.CostEstimate(
            flops=2 * heads * rows * depth * width, bytes_accessed=10 * MIB, transcendentals=0
        ),
        name="key_terms",
    )(grads, mask, scaled, *after)


def last_kernel(pieces, queries, weights, query_grad, weight_grad):
    summed = pieces[0].astype(F32)
    for k in range(1, pieces.shape[0]):
        summed += pieces[k].astype(F32)
    mine = pieces.shape[1]
    first = (lax.axis_index("x") * NZ + lax.axis_index("z")) * mine
    every = weights[...].astype(F32)
    for k in range(mine):
        own = queries[first + k].astype(F32)
        dots = jnp.sum(summed[k] * own, axis=1, keepdims=True)
        weight_grad[k : k + 1, :] = jnp.broadcast_to(dots, (dots.shape[0], 128)).T[0:1]
        query_grad[:, k, :] = (summed[k] * column(every, first + k)).astype(BF16)


def last_sums(pieces, queries, weights):
    _, mine, rows, depth = pieces.shape
    return pl.pallas_call(
        last_kernel,
        in_specs=[HERE] * 3,
        out_specs=[HERE] * 2,
        out_shape=[
            jax.ShapeDtypeStruct((rows, mine, depth), BF16),
            jax.ShapeDtypeStruct((mine, rows), F32),
        ],
        compiler_params=SMALL,
        name="last_sums",
    )(pieces, queries, weights)


def sum_kernel(*refs, count):
    total = refs[0][...].astype(F32)
    for part in refs[1:count]:
        total += part[...].astype(F32)
    refs[-1][...] = total.astype(BF16)


def sum_parts(parts, after=()):
    return pl.pallas_call(
        functools.partial(sum_kernel, count=len(parts)),
        in_specs=[HERE] * (len(parts) + len(after)),
        out_specs=HERE,
        out_shape=jax.ShapeDtypeStruct(parts[0].shape, BF16),
        compiler_params=SMALL,
    )(*parts, *after)


def pair_kernel(keep, arrived, *rest):
    for r, out in enumerate(rest[-NY:]):
        out[...] = (keep[r].astype(F32) + arrived[r].astype(F32)).astype(BF16)


def sum_pair(keep, arrived, after):
    part = jax.ShapeDtypeStruct(keep.shape[1:], BF16)
    return pl.pallas_call(
        pair_kernel,
        in_specs=[HERE] * (2 + len(after)),
        out_specs=[HERE] * NY,
        out_shape=[part] * NY,
        compiler_params=SMALL,
    )(keep, arrived, *after)


def sum_over_heads(keep, send, after=()):
    arrived = rotate(send, "core", 1)
    pairs = sum_pair(keep, arrived, after)
    return [pairs[0]] + [rotate(pairs[r], "y", r) for r in (1, 3, 2)]


def per_device(
    main_queries, main_keys, log_sums, index_queries, index_weights, index_keys, loss_weights
):
    rows, heads, depth = index_queries.shape
    scale = main_queries.shape[2] ** (-0.5)
    keep, send = head_scores(
        jnp.transpose(main_queries, (1, 2, 0)),
        jnp.transpose(main_keys, (1, 2, 0)),
        log_sums.T,
        rows,
        scale,
    )
    turned = jnp.transpose(index_queries, (1, 0, 2))
    parts = sum_over_heads(keep, send, (turned,))
    expo, sums, mask, scaled = index_logits(turned, index_keys, index_weights)

    probs, stats = local_stats(sums, parts)
    everywhere = lax.all_to_all(stats, ("x", "z"), split_axis=0, concat_axis=0, tiled=True)
    grads, two = first_terms(
        expo, sums, probs, everywhere, loss_weights[None], mask, index_keys, 2
    )
    one = shift_terms(grads, mask, index_keys, 1)
    three = shift_terms(grads, mask, index_keys, 3, (one,))
    across = []
    for r, term in ((2, two), (1, one), (3, three)):
        across.append(rotate(term, "x", r))
    key_keep, key_send = key_terms(grads, mask, scaled, (three,))
    key_parts = sum_over_heads(key_keep, key_send)
    own = shift_terms(grads, mask, index_keys, 0)
    summed = sum_parts([own] + across, key_parts[:1])
    pieces = lax.all_to_all(
        summed.reshape(NZ, heads // (NX * NZ), rows, depth),
        "z",
        split_axis=0,
        concat_axis=0,
        tiled=True,
    )
    query_grad, weight_grad = last_sums(pieces, turned, index_weights)
    key_grad = sum_parts(key_parts)
    return query_grad, weight_grad.T, key_grad.T


def solution(mesh):
    fine = Mesh(mesh.devices.reshape(NY, NC, NX, NZ), ("y", "core", "x", "z"))
    head, ctx = ("y", "core"), ("x", "z")
    return jax.shard_map(
        per_device,
        mesh=fine,
        in_specs=(
            P(None, head, None),
            P(ctx, head, None),
            P(None, head),
            P(head, None, None),
            P(head, None),
            P(ctx, None),
            P(head),
        ),
        out_specs=(P(head, ctx, None), P(head, ctx), P(ctx, head)),
        check_vma=False,
    )
```
